512 devices in a mesh: sub: 16 (over z, core), dom: 32 (over y, x).
Axes of the slice: x: 4, y: 8, z: 8, core: 2. Of those that a mesh axis runs over, the one named last changes fastest.
Arguments:
- leaf_maps: bfloat16 [32, 16, 512, 512], P('dom', 'sub'), may hold values from -0.1875 to 0.1875
- edge_blocks: int32 [32, 16], P('dom'), may hold values from 0 to 15, each once within a row
- incoming: float32 [32, 16, 512, 256], P('dom', 'sub'), may hold values from -6 to 6
Outputs:
- parent_maps: bfloat16 [32, 16, 2048, 512], P('dom', 'sub')
- leaf_traces: float32 [32, 16, 512, 256], P('dom', 'sub')
The draws below stay inside these ranges and needn't reach their ends.
Inputs may be any that keep to these rules, and one draw needn't show every extreme that they name: `edge_blocks`: each row is a permutation of the 16 blocks.
All inputs are finite; a program needn't handle non-finite values.
Results may differ from the reference program's by a relative error of at most 0.0085.
Values may be sent and summed in bfloat16 or wider, within the bound.
No kernel may reach another device: no remote copies, remote signals or barrier semaphores. Data moves between devices by JAX's collectives and lax.ppermute only.
A program may use at most 64 MiB of HBM per device.

```python
import jax
import jax.numpy as jnp
from jax import lax

M = 512
EDGE = 128
RHS = 256
KTERMS = 4
SWEEPS = 2
BLOCKS = 16
DOMS = 32
LEAVES = 16


def block_levels(rng, dims, pieces, smallest, top_value):
    factor_of, own = 1.0, jax.random.fold_in(rng, 6)
    for axis_at, shards_of in pieces:
        draws = jnp.exp(jax.random.uniform(jax.random.fold_in(own, axis_at), (shards_of,), jnp.float32, smallest / len(pieces), top_value / len(pieces)))
        factor_of = factor_of * jnp.repeat(draws, dims[axis_at] // shards_of).reshape([-1 if axis == axis_at else 1 for axis in range(len(dims))])
    return factor_of


def scatter_about(rng, shape, width, most, pieces=(), kind=jnp.bfloat16):
    values = jax.random.normal(rng, shape, jnp.float32) * width
    if len(pieces) > 0:
        values = block_levels(rng, shape, pieces, -0.22, 0.18) * values
    return jnp.clip(values, min=-most, max=most).astype(kind)


def setup_inputs(seed: int = 0) -> dict:
    keys = jax.random.split(jax.random.key(seed), 4)
    return {
        "leaf_maps": scatter_about(keys[0], (DOMS, LEAVES, M, M), (2 * M) ** -0.5, 0.1875, ((0, 32), (1, 16))),
        "edge_blocks": jax.vmap(lambda own: jax.random.permutation(own, BLOCKS))(jax.random.split(keys[1], DOMS)).reshape((DOMS, BLOCKS)).astype(jnp.int32),
        "incoming": scatter_about(keys[2], (DOMS, LEAVES, M, RHS), 1.0, 6.0, ((0, 32), (1, 16)), jnp.float32),
    }


def merge_group(operands):
    blocks, coupling = operands
    wide = 4 * M
    eye_four = jnp.eye(4, dtype=jnp.float32)
    first = jnp.einsum('cij,cd->cidj', blocks.astype(jnp.float32), eye_four).reshape(wide, wide).astype(jnp.bfloat16)
    total = first.astype(jnp.float32)
    term = first
    for order in range(KTERMS):
        shuffled = term.reshape(BLOCKS, EDGE, wide)[coupling].reshape(4, M, wide)
        term = jnp.einsum('cij,cjn->cin', blocks.astype(jnp.float32), shuffled.astype(jnp.float32)).reshape(wide, wide).astype(jnp.bfloat16)
        total = total + term.astype(jnp.float32)
    return total.astype(jnp.bfloat16)


def reference(leaf_maps, edge_blocks, incoming):
    groups = LEAVES // 4
    grouped = leaf_maps.reshape(DOMS * groups, 4, M, M)
    couplings = jnp.repeat(edge_blocks, groups, axis=0)
    parents = lax.map(merge_group, (grouped, couplings))
    parent_maps = parents.reshape(DOMS * groups, 4 * M, 4, M).transpose(0, 2, 1, 3).reshape(DOMS, LEAVES, 4 * M, M)
    current = incoming
    for sweep in range(SWEEPS):
        stacked = current.astype(jnp.bfloat16).reshape(DOMS * groups, 4 * M, RHS)
        returned = lax.map(lambda pair: jnp.dot(pair[0], pair[1], preferred_element_type=jnp.float32), (parents, stacked))
        returned = returned.reshape(DOMS, LEAVES, M, RHS)
        from_left = jnp.roll(returned, 1, axis=0)[:, :, M // 2:]
        from_right = jnp.roll(returned, -1, axis=0)[:, :, :M // 2]
        current = incoming + jnp.concatenate([from_left, from_right], axis=2)
    flat_maps = leaf_maps.reshape(DOMS * LEAVES, M, M)
    flat_data = current.astype(jnp.bfloat16).reshape(DOMS * LEAVES, M, RHS)
    leaf_traces = lax.map(lambda pair: jnp.dot(pair[0], pair[1], preferred_element_type=jnp.float32), (flat_maps, flat_data))
    return parent_maps, leaf_traces.reshape(DOMS, LEAVES, M, RHS)
```

```python
import jax
import jax.numpy as jnp
from jax import lax
from jax.experimental import pallas as pl
from jax.experimental.pallas import tpu as pltpu
from jax.sharding import PartitionSpec as P

KTERMS = 4
EDGE = 128
NT = (((1,), (1,)), ((), ()))
BF16 = jnp.bfloat16
F32 = jnp.float32
VMEM = pl.BlockSpec(memory_space=pltpu.VMEM)
SMEM = pl.BlockSpec(memory_space=pltpu.SMEM)


def sub_partner(value, mask):
    size = lax.axis_size("sub")
    return lax.ppermute(value, "sub", [(i, i ^ mask) for i in range(size)])


def dom_partner(value, first):
    size = lax.axis_size("dom")
    pairs = []
    for low in range(first, first + size, 2):
        left, right = low % size, (low + 1) % size
        pairs += [(left, right), (right, left)]
    return lax.ppermute(value, "dom", pairs)


def split_kernel(x_ref, *piece_refs):
    position = lax.axis_index("sub") % 4
    turned = x_ref[...].T.astype(BF16)
    width = turned.shape[0] // 4
    for index in range(4):
        block = turned[index * width : (index + 1) * width]
        for r, piece in enumerate(piece_refs):
            @pl.when((position ^ r) == index)
            def _():
                for i in range(4):
                    piece[i] = block[:, i * EDGE : (i + 1) * EDGE]


def split_rhs(x):
    rows, cols = x.shape
    shape = jax.ShapeDtypeStruct((rows // EDGE, cols // 4, EDGE), BF16)
    return pl.pallas_call(
        split_kernel, out_shape=(shape,) * 4, in_specs=[VMEM], out_specs=(VMEM,) * 4
    )(x)


def swapped_in(given_refs, got_a, got_b, parity):
    def block(r, i):
        half, k = i // 2, i % 2
        a, b = got_a[r, k].astype(F32), got_b[r, k].astype(F32)
        even_pick = b if half == 0 else a
        odd_pick = a if half == 0 else b
        return given_refs[r][i].astype(F32) + jnp.where(parity == 0, even_pick, odd_pick)

    return block


def chain(edge_ref, map_refs, base_block, store, z_ref):
    position = lax.axis_index("sub") % 4
    maps = [ref for ref in map_refs]
    for step in range(KTERMS + 1):
        slot, before = step % 2, (step + 1) % 2
        for r in range(4):
            leaf = position ^ r
            parts = []
            for i in range(4):
                part = base_block(r, i)
                if step > 0:
                    part = part + z_ref[before, edge_ref[0, leaf * 4 + i]]
                parts.append(part.astype(BF16))
            operand = jnp.concatenate(parts, 1)
            out = lax.dot_general(operand, maps[r][...], NT, preferred_element_type=F32)
            for i in range(4):
                value = out[:, i * EDGE : (i + 1) * EDGE]
                if step == KTERMS:
                    store(r, i, value)
                else:
                    z_ref[slot, leaf * 4 + i] = value


def send_store(to_a, to_b, parity):
    def store(r, i, value):
        half, k = i // 2, i % 2
        value = value.astype(BF16)

        @pl.when(parity == half)
        def _():
            to_b[r, k] = value

        @pl.when(parity != half)
        def _():
            to_a[r, k] = value

    return store


def first_sweep_kernel(edge, m0, m1, m2, m3, g0, g1, g2, g3, to_a, to_b, z):
    parity = lax.axis_index("dom") % 2
    given = (g0, g1, g2, g3)
    chain(
        edge, (m0, m1, m2, m3), lambda r, i: given[r][i].astype(F32), send_store(to_a, to_b, parity), z
    )


def next_sweep_kernel(edge, m0, m1, m2, m3, g0, g1, g2, g3, got_a, got_b, to_a, to_b, v, z):
    parity = lax.axis_index("dom") % 2
    block = swapped_in((g0, g1, g2, g3), got_a, got_b, parity)
    for r in range(4):
        for i in range(4):
            v[r, i] = block(r, i).astype(BF16)
    chain(
        edge, (m0, m1, m2, m3), lambda r, i: v[r, i].astype(F32), send_store(to_a, to_b, parity), z
    )


def sweep(edge, maps, given, got):
    blocks, width, _ = given[0].shape
    sent = jax.ShapeDtypeStruct((4, blocks // 2, width, EDGE), BF16)
    scratch = [pltpu.VMEM((2, 4 * blocks, width, EDGE), F32)]
    args = (edge, *maps, *given)
    kernel = first_sweep_kernel
    if got is not None:
        args += got
        kernel = next_sweep_kernel
        scratch = [pltpu.VMEM((4, blocks, width, EDGE), BF16)] + scratch
    return pl.pallas_call(
        kernel,
        out_shape=(sent, sent),
        in_specs=[SMEM] + [VMEM] * (len(args) - 1),
        out_specs=(VMEM, VMEM),
        scratch_shapes=scratch,
    )(*args)


def join_kernel(g0, g1, g2, g3, got_a, got_b, *out_refs):
    parity = lax.axis_index("dom") % 2
    block = swapped_in((g0, g1, g2, g3), got_a, got_b, parity)
    for r in range(4):
        for i in range(4):
            out_refs[r][i] = block(r, i).astype(BF16)


def join(given, got):
    shape = jax.ShapeDtypeStruct(given[0].shape, BF16)
    return pl.pallas_call(
        join_kernel, out_shape=(shape,) * 4, in_specs=[VMEM] * 6, out_specs=(VMEM,) * 4
    )(*given, *got)


def leaf_kernel(own, u0, u1, u2, u3, out, turned):
    position = lax.axis_index("sub") % 4
    width = u0.shape[1]
    for r, u in enumerate((u0, u1, u2, u3)):
        rows = pl.ds(pl.multiple_of((position ^ r) * width, width), width)
        for i in range(4):
            turned[rows, i * EDGE : (i + 1) * EDGE] = u[i]
    out[...] = lax.dot_general(own[...], turned[...], NT, preferred_element_type=F32)


def leaf_product(own, pieces):
    blocks, width, _ = pieces[0].shape
    return pl.pallas_call(
        leaf_kernel,
        out_shape=jax.ShapeDtypeStruct((own.shape[0], 4 * width), F32),
        in_specs=[VMEM] * 5,
        out_specs=VMEM,
        scratch_shapes=[pltpu.VMEM((4 * width, blocks * EDGE), BF16)],
    )(own, *pieces)


def apply_once(edge_ref, map_refs, source, target):
    position = lax.axis_index("sub") % 4
    for r in range(4):
        leaf = position ^ r
        operand = jnp.concatenate([source[edge_ref[0, leaf * 4 + i]] for i in range(4)], 0)
        out = jnp.dot(map_refs[r][...], operand, preferred_element_type=F32)
        if r == 0:
            out = out + map_refs[0][...].astype(F32)
        for i in range(4):
            target[leaf * 4 + i] = out[i * EDGE : (i + 1) * EDGE].astype(BF16)


def merge_first_kernel(edge, m0, m1, m2, m3, out, work):
    position = lax.axis_index("sub") % 4
    out[...] = jnp.zeros_like(out)
    for i in range(4):
        out[position * 4 + i] = m0[i * EDGE : (i + 1) * EDGE]
    apply_once(edge, (m0, m1, m2, m3), out, work)
    apply_once(edge, (m0, m1, m2, m3), work, out)


def merge_next_kernel(edge, m0, m1, m2, m3, source, out, work):
    apply_once(edge, (m0, m1, m2, m3), source, work)
    apply_once(edge, (m0, m1, m2, m3), work, out)


def merge(edge, maps, source):
    width = maps[0].shape[0]
    shape = (4 * width // EDGE, EDGE, width)
    args = (edge, *maps) + (() if source is None else (source,))
    return pl.pallas_call(
        merge_first_kernel if source is None else merge_next_kernel,
        out_shape=jax.ShapeDtypeStruct(shape, BF16),
        in_specs=[SMEM] + [VMEM] * (len(args) - 1),
        out_specs=VMEM,
        scratch_shapes=[pltpu.VMEM(shape, BF16)],
    )(*args)


def per_device(leaf_maps, edge, incoming):
    own = leaf_maps[0, 0]
    width = own.shape[0]
    across = sub_partner(own, 2)
    beside = sub_partner(own, 1)
    mine = split_rhs(incoming[0, 0])
    given = (mine[0],) + tuple(sub_partner(mine[r], r) for r in (1, 2, 3))
    maps = (own, beside, across, sub_partner(across, 1))

    def swap(sent):
        return dom_partner(sent[0], 0), dom_partner(sent[1], 1)

    sent = sweep(edge, maps, given, None)
    got = swap(sent)
    half_merged = merge(edge, maps, None)
    sent = sweep(edge, maps, given, got)
    got = swap(sent)
    merged = merge(edge, maps, half_merged)
    pieces = join(given, got)
    pieces = (pieces[0],) + tuple(sub_partner(pieces[r], r) for r in (1, 2, 3))
    leaf_out = leaf_product(own, pieces)
    return merged.reshape(1, 1, 4 * width, width), leaf_out[None, None]


def solution(mesh):
    placed = (P("dom", "sub", None, None), P("dom", None), P("dom", "sub", None, None))
    return jax.shard_map(
        per_device,
        mesh=mesh,
        in_specs=placed,
        out_specs=(P("dom", "sub", None, None), P("dom", "sub", None, None)),
        check_vma=False,
    )
```

```python
import jax
import jax.numpy as jnp
from jax import lax
from jax.experimental import pallas as pl
from jax.experimental.pallas import tpu as pltpu
from jax.sharding import PartitionSpec as P


KTERMS = 4
EDGE = 128
NT = (((1,), (1,)), ((), ()))
BF16 = jnp.bfloat16
F32 = jnp.float32
VMEM = pl.BlockSpec(memory_space=pltpu.VMEM)
EMPTY = pltpu.VMEM((8, 128), F32)
SMEM = pl.BlockSpec(memory_space=pltpu.SMEM)


def near(value):
    return pltpu.with_memory_space_constraint(value, pltpu.VMEM)


def call(kernel, results, args, scratch=(), edge=None):
    specs = [VMEM] * len(args)
    args = list(args)
    if edge is not None:
        specs, args = [SMEM] + specs, [edge] + args
    many = isinstance(results, tuple)
    made = pl.pallas_call(
        kernel,
        out_shape=results,
        in_specs=specs,
        out_specs=(VMEM,) * len(results) if many else VMEM,
        scratch_shapes=list(scratch),
        compiler_params=pltpu.CompilerParams(vmem_limit_bytes=16 << 20),
    )(*args)
    if many:
        return tuple(near(m) for m in made)
    return near(made) if isinstance(results, type(EMPTY)) else made


def sub_partner(value, mask):
    size = lax.axis_size("sub")
    return near(lax.ppermute(value, "sub", [(i, i ^ mask) for i in range(size)]))


def dom_partner(value, first):
    size = lax.axis_size("dom")
    pairs = []
    for low in range(first, first + size, 2):
        left, right = low % size, (low + 1) % size
        pairs += [(left, right), (right, left)]
    return near(lax.ppermute(value, "dom", pairs))


def split_kernel(edge_ref, own_ref, x_ref, edge_out, own_out, *refs):
    piece_refs, sem = refs[:4], refs[4]
    copy = pltpu.make_async_copy(own_ref, own_out, sem)
    copy.start()
    for k in range(edge_ref.shape[1]):
        edge_out[0, k] = edge_ref[0, k]
    position = lax.axis_index("sub") % 4
    turned = x_ref[...].T.astype(BF16)
    width = turned.shape[0] // 4
    for index in range(4):
        block = turned[index * width : (index + 1) * width]
        for r, piece in enumerate(piece_refs):
            @pl.when((position ^ r) == index)
            def _():
                for i in range(4):
                    piece[i] = block[:, i * EDGE : (i + 1) * EDGE]
    copy.wait()


def split_rhs(edge, own, x):
    rows, cols = x.shape
    piece = pltpu.VMEM((rows // EDGE, cols // 4, EDGE), BF16)
    edge, own, *pieces = pl.pallas_call(
        split_kernel,
        out_shape=(pltpu.SMEM(edge.shape, jnp.int32), pltpu.VMEM(own.shape, BF16)) + (piece,) * 4,
        in_specs=[SMEM, pl.BlockSpec(memory_space=pl.ANY), VMEM],
        out_specs=(SMEM,) + (VMEM,) * 5,
        scratch_shapes=[pltpu.SemaphoreType.DMA],
        compiler_params=pltpu.CompilerParams(vmem_limit_bytes=16 << 20),
    )(edge, own, x)
    edge = pltpu.with_memory_space_constraint(edge, pltpu.SMEM)
    return edge, near(own), [near(p) for p in pieces]


def swapped_in(given_refs, got_a, got_b, parity):
    def block(r, i):
        half, k = i // 2, i % 2
        a, b = got_a[r, k].astype(F32), got_b[r, k].astype(F32)
        even_pick = b if half == 0 else a
        odd_pick = a if half == 0 else b
        return given_refs[r][i].astype(F32) + jnp.where(parity == 0, even_pick, odd_pick)

    return block


def chain(edge_ref, turned, base_block, store, z_ref):
    position = lax.axis_index("sub") % 4
    for step in range(KTERMS + 1):
        slot, before = step % 2, (step + 1) % 2
        for r in range(4):
            leaf = position ^ r
            parts = []
            for i in range(4):
                part = base_block(r, i)
                if step > 0:
                    part = part + z_ref[before, edge_ref[0, leaf * 4 + i]]
                parts.append(part.astype(BF16))
            operand = jnp.concatenate(parts, 1)
            out = jnp.dot(operand, turned[r], preferred_element_type=F32)
            for i in range(4):
                value = out[:, i * EDGE : (i + 1) * EDGE]
                if step == KTERMS:
                    store(r, i, value)
                else:
                    z_ref[slot, leaf * 4 + i] = value


def send_store(to_a, to_b, parity):
    def store(r, i, value):
        half, k = i // 2, i % 2
        value = value.astype(BF16)

        @pl.when(parity == half)
        def _():
            to_b[r, k] = value

        @pl.when(parity != half)
        def _():
            to_a[r, k] = value

    return store


def first_sweep_kernel(edge, m0, m1, m2, m3, g0, g1, g2, g3, to_a, to_b, turned, z):
    parity = lax.axis_index("dom") % 2
    given = (g0, g1, g2, g3)
    for r, m in enumerate((m0, m1, m2, m3)):
        turned[r] = m[...].T
    chain(
        edge, turned, lambda r, i: given[r][i].astype(F32), send_store(to_a, to_b, parity), z
    )


def next_sweep_kernel(edge, turned, g0, g1, g2, g3, got_a, got_b, to_a, to_b, v, z):
    parity = lax.axis_index("dom") % 2
    block = swapped_in((g0, g1, g2, g3), got_a, got_b, parity)
    for r in range(4):
        for i in range(4):
            v[r, i] = block(r, i).astype(BF16)
    chain(
        edge, turned, lambda r, i: v[r, i].astype(F32), send_store(to_a, to_b, parity), z
    )


def first_sweep(edge, maps, given):
    blocks, width, _ = given[0].shape
    sent = pltpu.VMEM((4, blocks // 2, width, EDGE), BF16)
    turned = pltpu.VMEM((4,) + maps[0].shape, BF16)
    z = pltpu.VMEM((2, 4 * blocks, width, EDGE), F32)
    return call(first_sweep_kernel, (sent, sent, turned), (*maps, *given), (z,), edge)


def next_sweep(edge, turned, given, got):
    blocks, width, _ = given[0].shape
    sent = pltpu.VMEM((4, blocks // 2, width, EDGE), BF16)
    v = pltpu.VMEM((4, blocks, width, EDGE), BF16)
    z = pltpu.VMEM((2, 4 * blocks, width, EDGE), F32)
    return call(next_sweep_kernel, (sent, sent), (turned, *given, *got), (v, z), edge)


def join_kernel(g0, g1, g2, g3, got_a, got_b, *out_refs):
    parity = lax.axis_index("dom") % 2
    block = swapped_in((g0, g1, g2, g3), got_a, got_b, parity)
    for r in range(4):
        for i in range(4):
            out_refs[r][i] = block(r, i).astype(BF16)


def join(given, got):
    return call(join_kernel, (pltpu.VMEM(given[0].shape, BF16),) * 4, (*given, *got))


def leaf_kernel(own, u0, u1, u2, u3, out, turned):
    position = lax.axis_index("sub") % 4
    width = u0.shape[1]
    for r, u in enumerate((u0, u1, u2, u3)):
        rows = pl.ds(pl.multiple_of((position ^ r) * width, width), width)
        for i in range(4):
            turned[rows, i * EDGE : (i + 1) * EDGE] = u[i]
    out[...] = lax.dot_general(own[...], turned[...], NT, preferred_element_type=F32)


def leaf_product(own, pieces):
    blocks, width, _ = pieces[0].shape
    result = jax.ShapeDtypeStruct((own.shape[0], 4 * width), F32)
    turned = pltpu.VMEM((4 * width, blocks * EDGE), BF16)
    return call(leaf_kernel, result, (own, *pieces), (turned,))


def apply_once(edge_ref, map_refs, source, target):
    position = lax.axis_index("sub") % 4
    for r in range(4):
        leaf = position ^ r
        operand = jnp.concatenate([source[edge_ref[0, leaf * 4 + i]] for i in range(4)], 0)
        out = jnp.dot(map_refs[r][...], operand, preferred_element_type=F32)
        if r == 0:
            out = out + map_refs[0][...].astype(F32)
        for i in range(4):
            target[leaf * 4 + i] = out[i * EDGE : (i + 1) * EDGE].astype(BF16)


def merge_first_kernel(edge, m0, m1, m2, m3, out, work):
    position = lax.axis_index("sub") % 4
    out[...] = jnp.zeros_like(out)
    for i in range(4):
        out[position * 4 + i] = m0[i * EDGE : (i + 1) * EDGE]
    apply_once(edge, (m0, m1, m2, m3), out, work)
    apply_once(edge, (m0, m1, m2, m3), work, out)


def merge_next_kernel(edge, m0, m1, m2, m3, source, out, work):
    apply_once(edge, (m0, m1, m2, m3), source, work)
    apply_once(edge, (m0, m1, m2, m3), work, out)


def merge(edge, maps, source):
    width = maps[0].shape[0]
    shape = (4 * width // EDGE, EDGE, width)
    work = pltpu.VMEM(shape, BF16)
    if source is None:
        return call(merge_first_kernel, work, maps, (work,), edge)
    result = jax.ShapeDtypeStruct(shape, BF16)
    return call(merge_next_kernel, result, (*maps, source), (work,), edge)


def per_device(leaf_maps, edge, incoming):
    return steps(leaf_maps[0, 0], edge, incoming[0, 0])


def steps(own, edge, incoming):
    width = own.shape[0]
    across = sub_partner(own, 2)
    edge, own_near, mine = split_rhs(edge, own, near(incoming))
    given = [mine[0]]
    beside = sub_partner(own, 1)
    for r in (1, 2, 3):
        given.append(sub_partner(mine[r], r))
    opposite = sub_partner(across, 1)
    maps = (own_near, beside, across, opposite)

    def swap(sent):
        far = dom_partner(sent[1], 1)
        return dom_partner(sent[0], 0), far

    *sent, turned = first_sweep(edge, maps, given)
    got = swap(sent)
    half_merged = merge(edge, maps, None)
    sent = next_sweep(edge, turned, given, got)
    got = swap(sent)
    merged = merge(edge, maps, half_merged)
    mine = join(given, got)
    pieces = [mine[0]]
    for r in (1, 2, 3):
        pieces.append(sub_partner(mine[r], r))
    leaf_out = leaf_product(own_near, pieces)
    return merged.reshape(1, 1, 4 * width, width), leaf_out[None, None]


def solution(mesh):
    placed = (P("dom", "sub", None, None), P("dom", None), P("dom", "sub", None, None))
    return jax.shard_map(
        per_device,
        mesh=mesh,
        in_specs=placed,
        out_specs=(P("dom", "sub", None, None), P("dom", "sub", None, None)),
        check_vma=False,
    )
```

```python
import jax
import jax.numpy as jnp
from jax import lax
from jax.experimental import pallas as pl
from jax.experimental.pallas import tpu as pltpu
from jax.sharding import PartitionSpec as P


KTERMS = 4
EDGE = 128
NT = (((1,), (1,)), ((), ()))
BF16 = jnp.bfloat16
F32 = jnp.float32
VMEM = pl.BlockSpec(memory_space=pltpu.VMEM)
EMPTY = pltpu.VMEM((8, 128), F32)
SMEM = pl.BlockSpec(memory_space=pltpu.SMEM)


def near(value):
    return pltpu.with_memory_space_constraint(value, pltpu.VMEM)


def call(kernel, results, args, scratch=(), edge=None):
    specs = [VMEM] * len(args)
    args = list(args)
    if edge is not None:
        specs, args = [SMEM] + specs, [edge] + args
    many = isinstance(results, tuple)
    made = pl.pallas_call(
        kernel,
        out_shape=results,
        in_specs=specs,
        out_specs=(VMEM,) * len(results) if many else VMEM,
        scratch_shapes=list(scratch),
        compiler_params=pltpu.CompilerParams(vmem_limit_bytes=16 << 20),
    )(*args)
    if many:
        return tuple(near(m) for m in made)
    return near(made) if isinstance(results, type(EMPTY)) else made


def sub_partner(value, mask):
    size = lax.axis_size("sub")
    return near(lax.ppermute(value, "sub", [(i, i ^ mask) for i in range(size)]))


def dom_partner(value, first):
    size = lax.axis_size("dom")
    pairs = []
    for low in range(first, first + size, 2):
        left, right = low % size, (low + 1) % size
        pairs += [(left, right), (right, left)]
    return near(lax.ppermute(value, "dom", pairs))


def group_exchange(value):
    size = lax.axis_size("sub")
    groups = [list(range(g, g + 4)) for g in range(0, size, 4)]
    return near(lax.all_to_all(value, "sub", 0, 0, axis_index_groups=groups))


def split_kernel(edge_in, own_in, x_in, edge_out, own_out, pieces, x_ref, sems):
    fetch = pltpu.make_async_copy(x_in, x_ref, sems.at[0])
    others = [
        pltpu.make_async_copy(edge_in, edge_out, sems.at[1]),
        pltpu.make_async_copy(own_in, own_out, sems.at[2]),
    ]
    for copy in [fetch] + others:
        copy.start()
    fetch.wait()
    turned = x_ref[...].T.astype(BF16)
    width = turned.shape[0] // 4
    for k in range(4):
        for i in range(4):
            pieces[k, i] = turned[k * width : (k + 1) * width, i * EDGE : (i + 1) * EDGE]
    for copy in others:
        copy.wait()


def split_rhs(edge, own, x):
    rows, cols = x.shape
    edge, own, pieces = pl.pallas_call(
        split_kernel,
        out_shape=(
            pltpu.SMEM(edge.shape, jnp.int32),
            pltpu.VMEM(own.shape, BF16),
            pltpu.VMEM((4, rows // EDGE, cols // 4, EDGE), BF16),
        ),
        in_specs=[pl.BlockSpec(memory_space=pltpu.HBM)] * 3,
        out_specs=(SMEM, VMEM, VMEM),
        scratch_shapes=[pltpu.VMEM(x.shape, F32), pltpu.SemaphoreType.DMA((3,))],
        compiler_params=pltpu.CompilerParams(vmem_limit_bytes=16 << 20),
    )(*(pltpu.with_memory_space_constraint(a, pltpu.HBM) for a in (edge, own, x)))
    return pltpu.with_memory_space_constraint(edge, pltpu.SMEM), near(own), near(pieces)


def swapped_in(given, got_a, got_b):
    position, parity = lax.axis_index("sub") % 4, lax.axis_index("dom") % 2

    def block(r, i):
        half, k = i // 2, i % 2
        a, b = got_a[r, k].astype(F32), got_b[r, k].astype(F32)
        even_pick = b if half == 0 else a
        odd_pick = a if half == 0 else b
        return given[position ^ r, i].astype(F32) + jnp.where(parity == 0, even_pick, odd_pick)

    return block


def chain(edge_ref, turned, base_block, store, z_ref):
    position = lax.axis_index("sub") % 4
    for step in range(KTERMS + 1):
        slot, before = step % 2, (step + 1) % 2
        for r in range(4):
            leaf = position ^ r
            parts = []
            for i in range(4):
                part = base_block(r, i)
                if step > 0:
                    part = part + z_ref[before, edge_ref[0, leaf * 4 + i]]
                parts.append(part.astype(BF16))
            operand = jnp.concatenate(parts, 1)
            out = jnp.dot(operand, turned[r], preferred_element_type=F32)
            for i in range(4):
                value = out[:, i * EDGE : (i + 1) * EDGE]
                if step == KTERMS:
                    store(r, i, value)
                else:
                    z_ref[slot, leaf * 4 + i] = value


def send_store(to_a, to_b, parity):
    def store(r, i, value):
        half, k = i // 2, i % 2
        value = value.astype(BF16)

        @pl.when(parity == half)
        def _():
            to_b[r, k] = value

        @pl.when(parity != half)
        def _():
            to_a[r, k] = value

    return store


def first_sweep_kernel(edge, m0, m1, m2, m3, given, to_a, to_b, turned, z):
    position, parity = lax.axis_index("sub") % 4, lax.axis_index("dom") % 2
    for r, m in enumerate((m0, m1, m2, m3)):
        turned[r] = m[...].T
    base = lambda r, i: given[position ^ r, i].astype(F32)
    chain(edge, turned, base, send_store(to_a, to_b, parity), z)


def next_sweep_kernel(edge, turned, given, got_a, got_b, to_a, to_b, v, z):
    parity = lax.axis_index("dom") % 2
    block = swapped_in(given, got_a, got_b)
    for r in range(4):
        for i in range(4):
            v[r, i] = block(r, i).astype(BF16)
    base = lambda r, i: v[r, i].astype(F32)
    chain(edge, turned, base, send_store(to_a, to_b, parity), z)


def first_sweep(edge, maps, given):
    _, blocks, width, _ = given.shape
    sent = pltpu.VMEM((4, blocks // 2, width, EDGE), BF16)
    turned = pltpu.VMEM((4,) + maps[0].shape, BF16)
    z = pltpu.VMEM((2, 4 * blocks, width, EDGE), F32)
    return call(first_sweep_kernel, (sent, sent, turned), (*maps, given), (z,), edge)


def next_sweep(edge, turned, given, got):
    _, blocks, width, _ = given.shape
    sent = pltpu.VMEM((4, blocks // 2, width, EDGE), BF16)
    v = pltpu.VMEM(given.shape, BF16)
    z = pltpu.VMEM((2, 4 * blocks, width, EDGE), F32)
    return call(next_sweep_kernel, (sent, sent), (turned, given, *got), (v, z), edge)


def join_kernel(given, got_a, got_b, out):
    position = lax.axis_index("sub") % 4
    block = swapped_in(given, got_a, got_b)
    for r in range(4):
        for i in range(4):
            out[position ^ r, i] = block(r, i).astype(BF16)


def join(given, got):
    return call(join_kernel, pltpu.VMEM(given.shape, BF16), (given, *got))


def leaf_kernel(own, pieces, out, turned):
    width = pieces.shape[2]
    for k in range(4):
        for i in range(4):
            turned[k * width : (k + 1) * width, i * EDGE : (i + 1) * EDGE] = pieces[k, i]
    out[...] = lax.dot_general(own[...], turned[...], NT, preferred_element_type=F32)


def leaf_product(own, pieces):
    _, blocks, width, _ = pieces.shape
    result = jax.ShapeDtypeStruct((own.shape[0], 4 * width), F32)
    turned = pltpu.VMEM((4 * width, blocks * EDGE), BF16)
    return call(leaf_kernel, result, (own, pieces), (turned,))


def apply_once(edge_ref, map_refs, source, target):
    position = lax.axis_index("sub") % 4
    for r in range(4):
        leaf = position ^ r
        operand = jnp.concatenate([source[edge_ref[0, leaf * 4 + i]] for i in range(4)], 0)
        out = jnp.dot(map_refs[r][...], operand, preferred_element_type=F32)
        if r == 0:
            out = out + map_refs[0][...].astype(F32)
        for i in range(4):
            target[leaf * 4 + i] = out[i * EDGE : (i + 1) * EDGE].astype(BF16)


def merge_first_kernel(edge, m0, m1, m2, m3, out, work):
    position = lax.axis_index("sub") % 4
    out[...] = jnp.zeros_like(out)
    for i in range(4):
        out[position * 4 + i] = m0[i * EDGE : (i + 1) * EDGE]
    apply_once(edge, (m0, m1, m2, m3), out, work)
    apply_once(edge, (m0, m1, m2, m3), work, out)


def merge_next_kernel(edge, m0, m1, m2, m3, source, out, work):
    apply_once(edge, (m0, m1, m2, m3), source, work)
    apply_once(edge, (m0, m1, m2, m3), work, out)


def merge(edge, maps, source):
    width = maps[0].shape[0]
    work = pltpu.VMEM((4 * width // EDGE, EDGE, width), BF16)
    if source is None:
        return call(merge_first_kernel, work, maps, (work,), edge)
    return call(merge_next_kernel, work, (*maps, source), (work,), edge)


def store_kernel(value, out, sem):
    copy = pltpu.make_async_copy(value, out, sem)
    copy.start()
    copy.wait()


def store(value):
    return pl.pallas_call(
        store_kernel,
        out_shape=jax.ShapeDtypeStruct(value.shape, value.dtype),
        in_specs=[VMEM],
        out_specs=pl.BlockSpec(memory_space=pltpu.HBM),
        scratch_shapes=[pltpu.SemaphoreType.DMA],
        compiler_params=pltpu.CompilerParams(vmem_limit_bytes=1 << 20),
    )(value)


def per_device(leaf_maps, edge, incoming):
    return steps(leaf_maps[0, 0], edge, incoming[0, 0])


def steps(own, edge, incoming):
    width = own.shape[0]
    across = sub_partner(own, 2)
    edge, own_near, mine = split_rhs(edge, own, incoming)
    beside = sub_partner(own, 1)
    given = group_exchange(mine)
    opposite = sub_partner(across, 1)
    maps = (own_near, beside, across, opposite)

    def swap(sent):
        far = dom_partner(sent[1], 1)
        return dom_partner(sent[0], 0), far

    *sent, turned = first_sweep(edge, maps, given)
    got = swap(sent)
    merged = merge(edge, maps, None)
    sent = next_sweep(edge, turned, given, got)
    got = swap(sent)
    merged = merge(edge, maps, merged)
    mine = join(given, got)
    pieces = group_exchange(mine)
    merged = store(merged)
    leaf_out = leaf_product(own_near, pieces)
    return merged.reshape(1, 1, 4 * width, width), leaf_out[None, None]


def solution(mesh):
    placed = (P("dom", "sub", None, None), P("dom", None), P("dom", "sub", None, None))
    return jax.shard_map(
        per_device,
        mesh=mesh,
        in_specs=placed,
        out_specs=(P("dom", "sub", None, None), P("dom", "sub", None, None)),
        check_vma=False,
    )
```

```python
import jax
import jax.numpy as jnp
from jax import lax
from jax.experimental import pallas as pl
from jax.experimental.pallas import tpu as pltpu
from jax.sharding import PartitionSpec as P


KTERMS = 4
EDGE = 128
NT = (((1,), (1,)), ((), ()))
BF16 = jnp.bfloat16
F32 = jnp.float32
VMEM = pl.BlockSpec(memory_space=pltpu.VMEM)
EMPTY = pltpu.VMEM((8, 128), F32)
SMEM = pl.BlockSpec(memory_space=pltpu.SMEM)


def near(value):
    return pltpu.with_memory_space_constraint(value, pltpu.VMEM)


def call(kernel, results, args, scratch=(), edge=None):
    specs = [VMEM] * len(args)
    args = list(args)
    if edge is not None:
        specs, args = [SMEM] + specs, [edge] + args
    many = isinstance(results, tuple)
    made = pl.pallas_call(
        kernel,
        out_shape=results,
        in_specs=specs,
        out_specs=(VMEM,) * len(results) if many else VMEM,
        scratch_shapes=list(scratch),
        compiler_params=pltpu.CompilerParams(vmem_limit_bytes=16 << 20),
    )(*args)
    if many:
        return tuple(near(m) for m in made)
    return near(made) if isinstance(results, type(EMPTY)) else made


def sub_partner(value, mask):
    size = lax.axis_size("sub")
    return near(lax.ppermute(value, "sub", [(i, i ^ mask) for i in range(size)]))


def dom_pairs(first):
    size = lax.axis_size("dom")
    pairs = []
    for low in range(first, first + size, 2):
        left, right = low % size, (low + 1) % size
        pairs += [(left, right), (right, left)]
    return pairs


def dom_partner(value, first):
    return near(lax.ppermute(value, "dom", dom_pairs(first)))


def cross_partner(value, first, mask):
    size = lax.axis_size("dom")
    pairs = [
        (s * size + a, (s ^ mask) * size + b)
        for s in range(lax.axis_size("sub"))
        for a, b in dom_pairs(first)
    ]
    return near(lax.ppermute(value, ("sub", "dom"), pairs))


def group_exchange(value):
    size = lax.axis_size("sub")
    groups = [list(range(g, g + 4)) for g in range(0, size, 4)]
    return near(lax.all_to_all(value, "sub", 0, 0, axis_index_groups=groups))


def split_kernel(edge_in, own_in, x_in, edge_out, own_out, pieces, kept, x_ref, sems):
    fetch = pltpu.make_async_copy(x_in, x_ref, sems.at[0])
    others = [
        pltpu.make_async_copy(edge_in, edge_out, sems.at[1]),
        pltpu.make_async_copy(own_in, own_out, sems.at[2]),
    ]
    for copy in [fetch] + others:
        copy.start()
    fetch.wait()
    turned = x_ref[...].T.astype(BF16)
    width = turned.shape[0] // 4
    for k in range(4):
        for i in range(4):
            block = turned[k * width : (k + 1) * width, i * EDGE : (i + 1) * EDGE]
            pieces[k, i] = block
            kept[k, i] = block
    for copy in others:
        copy.wait()


def split_rhs(edge, own, x):
    rows, cols = x.shape
    piece = pltpu.VMEM((4, rows // EDGE, cols // 4, EDGE), BF16)
    edge, own, pieces, kept = pl.pallas_call(
        split_kernel,
        out_shape=(
            pltpu.SMEM(edge.shape, jnp.int32),
            pltpu.VMEM(own.shape, BF16),
            piece,
            piece,
        ),
        in_specs=[pl.BlockSpec(memory_space=pltpu.HBM)] * 3,
        out_specs=(SMEM, VMEM, VMEM, VMEM),
        scratch_shapes=[pltpu.VMEM(x.shape, F32), pltpu.SemaphoreType.DMA((3,))],
        compiler_params=pltpu.CompilerParams(vmem_limit_bytes=16 << 20),
    )(*(pltpu.with_memory_space_constraint(a, pltpu.HBM) for a in (edge, own, x)))
    edge = pltpu.with_memory_space_constraint(edge, pltpu.SMEM)
    return edge, near(own), near(pieces), near(kept)


def swapped_in(given, got_a, got_b):
    position, parity = lax.axis_index("sub") % 4, lax.axis_index("dom") % 2

    def block(r, i):
        half, k = i // 2, i % 2
        a, b = got_a[r, k].astype(F32), got_b[r, k].astype(F32)
        even_pick = b if half == 0 else a
        odd_pick = a if half == 0 else b
        return given[position ^ r, i].astype(F32) + jnp.where(parity == 0, even_pick, odd_pick)

    return block


def chain(edge_ref, turned_pairs, base_block, store, z_ref):
    position = lax.axis_index("sub") % 4
    for step in range(KTERMS + 1):
        slot, before = step % 2, (step + 1) % 2
        for r in range(4):
            leaf = position ^ r
            parts = []
            for i in range(4):
                part = base_block(r, i)
                if step > 0:
                    part = part + z_ref[before, edge_ref[0, leaf * 4 + i]]
                parts.append(part.astype(BF16))
            operand = jnp.concatenate(parts, 1)
            turned = turned_pairs[r // 2][r % 2]
            out = jnp.dot(operand, turned, preferred_element_type=F32)
            for i in range(4):
                value = out[:, i * EDGE : (i + 1) * EDGE]
                if step == KTERMS:
                    store(r, i, value)
                else:
                    z_ref[slot, leaf * 4 + i] = value


def send_store(to_near, to_far, parity):
    def store(r, i, value):
        half, k = i // 2, i % 2
        value = value.astype(BF16)
        run = 4 // len(to_near)

        @pl.when(parity == half)
        def _():
            to_far[r // run][r % run, k] = value

        @pl.when(parity != half)
        def _():
            to_near[r // run][r % run, k] = value

    return store


def first_sweep_kernel(edge, here, m2, m3, given, to_a, to_b, come, z):
    position, parity = lax.axis_index("sub") % 4, lax.axis_index("dom") % 2
    for k, m in enumerate((m2, m3)):
        come[k] = m[...].T
    base = lambda r, i: given[position ^ r, i].astype(F32)
    chain(edge, (here, come), base, send_store((to_a,), (to_b,), parity), z)


def next_sweep_kernel(edge, here, come, given, got_a, got_b, n0, n2, f0, f2, v, z):
    parity = lax.axis_index("dom") % 2
    block = swapped_in(given, got_a, got_b)
    for r in range(4):
        for i in range(4):
            v[r, i] = block(r, i).astype(BF16)
    base = lambda r, i: v[r, i].astype(F32)
    chain(edge, (here, come), base, send_store((n0, n2), (f0, f2), parity), z)


def first_sweep(edge, here, m2, m3, given):
    _, blocks, width, _ = given.shape
    sent = pltpu.VMEM((4, blocks // 2, width, EDGE), BF16)
    come = pltpu.VMEM(here.shape, BF16)
    z = pltpu.VMEM((2, 4 * blocks, width, EDGE), F32)
    return call(first_sweep_kernel, (sent, sent, come), (here, m2, m3, given), (z,), edge)


def next_sweep(edge, here, come, given, got):
    _, blocks, width, _ = given.shape
    sent = pltpu.VMEM((2, blocks // 2, width, EDGE), BF16)
    v = pltpu.VMEM(given.shape, BF16)
    z = pltpu.VMEM((2, 4 * blocks, width, EDGE), F32)
    return call(next_sweep_kernel, (sent,) * 4, (here, come, given, *got), (v, z), edge)


def picked(near_ref, far_ref, leaf, i, parity):
    half, k = i // 2, i % 2
    return jnp.where(parity == half, far_ref[leaf, k].astype(F32), near_ref[leaf, k].astype(F32))


def join_kernel(n0, n2, f0, f2, out):
    parity = lax.axis_index("dom") % 2
    for k, refs in enumerate(((n0, f0), (n2, f2))):
        for i in range(4):
            out[k, i] = picked(*refs, 1, i, parity).astype(BF16)


def join(got):
    _, halves, width, _ = got[0].shape
    return call(join_kernel, pltpu.VMEM((2, 2 * halves, width, EDGE), BF16), got)


def leaf_kernel(own, kept, n0, n2, f0, f2, others, out, turned):
    position, parity = lax.axis_index("sub") % 4, lax.axis_index("dom") % 2
    width = kept.shape[2]
    for r in range(4):
        member = position ^ r
        rows = pl.ds(pl.multiple_of(member * width, width), width)
        for i in range(4):
            if r % 2 == 0:
                refs = (n0, f0) if r == 0 else (n2, f2)
                value = picked(*refs, 0, i, parity)
            else:
                value = others[r // 2, i].astype(F32)
            u = kept[member, i].astype(F32) + value
            turned[rows, i * EDGE : (i + 1) * EDGE] = u.astype(BF16)
    out[...] = lax.dot_general(own[...], turned[...], NT, preferred_element_type=F32)


def leaf_product(own, kept, got, others):
    _, blocks, width, _ = kept.shape
    result = jax.ShapeDtypeStruct((own.shape[0], 4 * width), F32)
    turned = pltpu.VMEM((4 * width, blocks * EDGE), BF16)
    return call(leaf_kernel, result, (own, kept, *got, others), (turned,))


def apply_once(edge_ref, map_refs, source, target, leaves=range(4)):
    position = lax.axis_index("sub") % 4
    for r in leaves:
        leaf = position ^ r
        operand = jnp.concatenate([source[edge_ref[0, leaf * 4 + i]] for i in range(4)], 0)
        out = jnp.dot(map_refs[r][...], operand, preferred_element_type=F32)
        if r == 0:
            out = out + map_refs[0][...].astype(F32)
        for i in range(4):
            target[leaf * 4 + i] = out[i * EDGE : (i + 1) * EDGE].astype(BF16)


def apply_first(edge_ref, m_ref, own_ref, r):
    position = lax.axis_index("sub") % 4
    parts = []
    for i in range(4):
        block = edge_ref[0, (position ^ r) * 4 + i]
        rows = own_ref[pl.ds(pl.multiple_of(block % 4 * EDGE, EDGE), EDGE), :]
        parts.append(jnp.where(block // 4 == position, rows, jnp.zeros_like(rows)))
    out = jnp.dot(m_ref[...], jnp.concatenate(parts, 0), preferred_element_type=F32)
    if r == 0:
        out = out + own_ref[...].astype(F32)
    return [out[i * EDGE : (i + 1) * EDGE].astype(BF16) for i in range(4)]


def early_kernel(edge, m0, m1, here, begun):
    for r, m in enumerate((m0, m1)):
        here[r] = m[...].T
        for i, value in enumerate(apply_first(edge, m, m0, r)):
            begun[r, i] = value


def early(edge, own, beside):
    here = pltpu.VMEM((2,) + own.shape, BF16)
    begun = pltpu.VMEM((2, 4, EDGE, own.shape[1]), BF16)
    return call(early_kernel, (here, begun), (own, beside), (), edge)


def merge_first_kernel(edge, m0, m1, m2, m3, begun, out, work):
    position = lax.axis_index("sub") % 4
    for r in range(2):
        for i in range(4):
            work[(position ^ r) * 4 + i] = begun[r, i]
    for r, m in ((2, m2), (3, m3)):
        for i, value in enumerate(apply_first(edge, m, m0, r)):
            work[(position ^ r) * 4 + i] = value
    apply_once(edge, (m0, m1, m2, m3), work, out)


def merge_next_kernel(edge, m0, m1, m2, m3, source, out, work, last, sems):
    maps = (m0, m1, m2, m3)
    position = lax.axis_index("sub") % 4
    apply_once(edge, maps, source, work)
    copies = []
    for r in range(4):
        apply_once(edge, maps, work, last, (r,))
        blocks = pl.ds((position ^ r) * 4, 4)
        copies.append(pltpu.make_async_copy(last.at[blocks], out.at[blocks], sems.at[r]))
        copies[-1].start()
    for copy in copies:
        copy.wait()


def merge_first(edge, maps, begun):
    width = maps[0].shape[0]
    work = pltpu.VMEM((4 * width // EDGE, EDGE, width), BF16)
    return call(merge_first_kernel, work, (*maps, begun), (work,), edge)


def merge_last(edge, maps, source):
    return pl.pallas_call(
        merge_next_kernel,
        out_shape=jax.ShapeDtypeStruct(source.shape, BF16),
        in_specs=[SMEM] + [VMEM] * 5,
        out_specs=pl.BlockSpec(memory_space=pltpu.HBM),
        scratch_shapes=[pltpu.VMEM(source.shape, BF16)] * 2 + [pltpu.SemaphoreType.DMA((4,))],
        compiler_params=pltpu.CompilerParams(vmem_limit_bytes=16 << 20),
    )(edge, *maps, source)


def per_device(leaf_maps, edge, incoming):
    return steps(leaf_maps[0, 0], edge, incoming[0, 0])


def steps(own, edge, incoming):
    width = own.shape[0]
    across = sub_partner(own, 2)
    edge, own_near, mine, kept = split_rhs(edge, own, incoming)
    beside = sub_partner(own, 1)
    here, begun = early(edge, own_near, beside)
    given = group_exchange(mine)
    opposite = sub_partner(across, 1)
    maps = (own_near, beside, across, opposite)

    def swap(sent):
        far = dom_partner(sent[1], 1)
        return dom_partner(sent[0], 0), far

    *sent, come = first_sweep(edge, here, across, opposite, given)
    got = swap(sent)
    merged = merge_first(edge, maps, begun)
    sent = next_sweep(edge, here, come, given, got)
    far2 = cross_partner(sent[3], 1, 2)
    far0 = dom_partner(sent[2], 1)
    near2 = cross_partner(sent[1], 0, 2)
    near0 = dom_partner(sent[0], 0)
    got = (near0, near2, far0, far2)
    merged = merge_last(edge, maps, merged)
    mine = join(got)
    others = sub_partner(mine, 1)
    leaf_out = leaf_product(own_near, kept, got, others)
    return merged.reshape(1, 1, 4 * width, width), leaf_out[None, None]


def solution(mesh):
    placed = (P("dom", "sub", None, None), P("dom", None), P("dom", "sub", None, None))
    return jax.shard_map(
        per_device,
        mesh=mesh,
        in_specs=placed,
        out_specs=(P("dom", "sub", None, None), P("dom", "sub", None, None)),
        check_vma=False,
    )
```

```python
import jax
import jax.numpy as jnp
from jax import lax
from jax.experimental import pallas as pl
from jax.experimental.pallas import tpu as pltpu
from jax.sharding import PartitionSpec as P


KTERMS = 4
EDGE = 128
NT = (((1,), (1,)), ((), ()))
BF16 = jnp.bfloat16
F32 = jnp.float32
VMEM = pl.BlockSpec(memory_space=pltpu.VMEM)
EMPTY = pltpu.VMEM((8, 128), F32)
SMEM = pl.BlockSpec(memory_space=pltpu.SMEM)


def near(value):
    return pltpu.with_memory_space_constraint(value, pltpu.VMEM)


def call(kernel, results, args, scratch=(), edge=None):
    specs = [VMEM] * len(args)
    args = list(args)
    if edge is not None:
        specs, args = [SMEM] + specs, [edge] + args
    many = isinstance(results, tuple)
    made = pl.pallas_call(
        kernel,
        out_shape=results,
        in_specs=specs,
        out_specs=(VMEM,) * len(results) if many else VMEM,
        scratch_shapes=list(scratch),
        compiler_params=pltpu.CompilerParams(vmem_limit_bytes=16 << 20),
    )(*args)
    if many:
        return tuple(near(m) for m in made)
    return near(made) if isinstance(results, type(EMPTY)) else made


def sub_partner(value, mask):
    size = lax.axis_size("sub")
    return near(lax.ppermute(value, "sub", [(i, i ^ mask) for i in range(size)]))


def dom_partner(value, first):
    size = lax.axis_size("dom")
    pairs = []
    for low in range(first, first + size, 2):
        left, right = low % size, (low + 1) % size
        pairs += [(left, right), (right, left)]
    return near(lax.ppermute(value, "dom", pairs))


def group_exchange(value):
    size = lax.axis_size("sub")
    groups = [list(range(g, g + 4)) for g in range(0, size, 4)]
    return near(lax.all_to_all(value, "sub", 0, 0, axis_index_groups=groups))


def split_kernel(edge_in, own_in, x_in, edge_out, own_out, pieces, x_ref, sems):
    fetch = pltpu.make_async_copy(x_in, x_ref, sems.at[0])
    others = [
        pltpu.make_async_copy(edge_in, edge_out, sems.at[1]),
        pltpu.make_async_copy(own_in, own_out, sems.at[2]),
    ]
    for copy in [fetch] + others:
        copy.start()
    fetch.wait()
    turned = x_ref[...].T.astype(BF16)
    width = turned.shape[0] // 4
    for k in range(4):
        for i in range(4):
            pieces[k, i] = turned[k * width : (k + 1) * width, i * EDGE : (i + 1) * EDGE]
    for copy in others:
        copy.wait()


def split_rhs(edge, own, x):
    rows, cols = x.shape
    edge, own, pieces = pl.pallas_call(
        split_kernel,
        out_shape=(
            pltpu.SMEM(edge.shape, jnp.int32),
            pltpu.VMEM(own.shape, BF16),
            pltpu.VMEM((4, rows // EDGE, cols // 4, EDGE), BF16),
        ),
        in_specs=[pl.BlockSpec(memory_space=pltpu.HBM)] * 3,
        out_specs=(SMEM, VMEM, VMEM),
        scratch_shapes=[pltpu.VMEM(x.shape, F32), pltpu.SemaphoreType.DMA((3,))],
        compiler_params=pltpu.CompilerParams(vmem_limit_bytes=16 << 20),
    )(*(pltpu.with_memory_space_constraint(a, pltpu.HBM) for a in (edge, own, x)))
    return pltpu.with_memory_space_constraint(edge, pltpu.SMEM), near(own), near(pieces)


def swapped_in(given, got_a, got_b):
    position, parity = lax.axis_index("sub") % 4, lax.axis_index("dom") % 2

    def block(r, i):
        half, k = i // 2, i % 2
        a, b = got_a[r, k].astype(F32), got_b[r, k].astype(F32)
        even_pick = b if half == 0 else a
        odd_pick = a if half == 0 else b
        return given[position ^ r, i].astype(F32) + jnp.where(parity == 0, even_pick, odd_pick)

    return block


def chain(edge_ref, turned, base_block, store, z_ref, known=()):
    position = lax.axis_index("sub") % 4
    for step in range(KTERMS + 1):
        slot, before = step % 2, (step + 1) % 2
        for r in range(4):
            leaf = position ^ r
            if step == 0 and r in known:
                continue
            parts = []
            for i in range(4):
                part = base_block(r, i)
                if step > 0:
                    part = part + z_ref[before, edge_ref[0, leaf * 4 + i]]
                parts.append(part.astype(BF16))
            operand = jnp.concatenate(parts, 1)
            out = jnp.dot(operand, turned[r][...], preferred_element_type=F32)
            for i in range(4):
                value = out[:, i * EDGE : (i + 1) * EDGE]
                if step == KTERMS:
                    store(r, i, value)
                else:
                    z_ref[slot, leaf * 4 + i] = value


def send_store(to_a, to_b, parity):
    def store(r, i, value):
        half, k = i // 2, i % 2
        value = value.astype(BF16)

        @pl.when(parity == half)
        def _():
            to_b[r, k] = value

        @pl.when(parity != half)
        def _():
            to_a[r, k] = value

    return store


def products_kernel(here, m2, given, t2, begun):
    position = lax.axis_index("sub") % 4
    t2[...] = m2[...].T
    for r, turned in enumerate((here.at[0], here.at[1], t2)):
        v = jnp.concatenate([given[position ^ r, i] for i in range(4)], 1)
        out = jnp.dot(v, turned[...], preferred_element_type=F32)
        for i in range(4):
            begun[r, i] = out[:, i * EDGE : (i + 1) * EDGE]


def products(here, m2, given):
    t2 = pltpu.VMEM(m2.shape, BF16)
    begun = pltpu.VMEM((3,) + given.shape[1:], F32)
    return call(products_kernel, (t2, begun), (here, m2, given))


def first_sweep_kernel(edge, here, t2, begun, m3, given, to_a, to_b, t3, z):
    position, parity = lax.axis_index("sub") % 4, lax.axis_index("dom") % 2
    t3[...] = m3[...].T
    for r in range(3):
        for i in range(4):
            z[0, (position ^ r) * 4 + i] = begun[r, i]
    base = lambda r, i: given[position ^ r, i].astype(F32)
    turned = (here.at[0], here.at[1], t2, t3)
    chain(edge, turned, base, send_store(to_a, to_b, parity), z, (0, 1, 2))


def next_sweep_kernel(edge, here, t2, t3, given, got_a, got_b, to_a, to_b, v, z):
    parity = lax.axis_index("dom") % 2
    block = swapped_in(given, got_a, got_b)
    for r in range(4):
        for i in range(4):
            v[r, i] = block(r, i).astype(BF16)
    base = lambda r, i: v[r, i].astype(F32)
    turned = (here.at[0], here.at[1], t2, t3)
    chain(edge, turned, base, send_store(to_a, to_b, parity), z)


def first_sweep(edge, here, t2, begun, m3, given):
    _, blocks, width, _ = given.shape
    sent = pltpu.VMEM((4, blocks // 2, width, EDGE), BF16)
    t3 = pltpu.VMEM(m3.shape, BF16)
    z = pltpu.VMEM((2, 4 * blocks, width, EDGE), F32)
    args = (here, t2, begun, m3, given)
    return call(first_sweep_kernel, (sent, sent, t3), args, (z,), edge)


def next_sweep(edge, here, t2, t3, given, got):
    _, blocks, width, _ = given.shape
    sent = pltpu.VMEM((4, blocks // 2, width, EDGE), BF16)
    v = pltpu.VMEM(given.shape, BF16)
    z = pltpu.VMEM((2, 4 * blocks, width, EDGE), F32)
    return call(next_sweep_kernel, (sent, sent), (here, t2, t3, given, *got), (v, z), edge)


def join_kernel(given, got_a, got_b, *out_refs):
    block = swapped_in(given, got_a, got_b)
    for r in range(4):
        for i in range(4):
            out_refs[r][i] = block(r, i).astype(BF16)


def join(given, got):
    return call(join_kernel, (pltpu.VMEM(given.shape[1:], BF16),) * 4, (given, *got))


def leaf_kernel(own, u0, u1, u2, u3, out, turned):
    position = lax.axis_index("sub") % 4
    width = u0.shape[1]
    for r, u in enumerate((u0, u1, u2, u3)):
        rows = pl.ds(pl.multiple_of((position ^ r) * width, width), width)
        for i in range(4):
            turned[rows, i * EDGE : (i + 1) * EDGE] = u[i]
    out[...] = lax.dot_general(own[...], turned[...], NT, preferred_element_type=F32)


def leaf_product(own, pieces):
    blocks, width, _ = pieces[0].shape
    result = jax.ShapeDtypeStruct((own.shape[0], 4 * width), F32)
    turned = pltpu.VMEM((4 * width, blocks * EDGE), BF16)
    return call(leaf_kernel, result, (own, *pieces), (turned,))


def apply_leaf(edge_ref, map_refs, source, r):
    leaf = (lax.axis_index("sub") % 4) ^ r
    operand = jnp.concatenate([source[edge_ref[0, leaf * 4 + i]] for i in range(4)], 0)
    out = jnp.dot(map_refs[r][...], operand, preferred_element_type=F32)
    if r == 0:
        out = out + map_refs[0][...].astype(F32)
    return [out[i * EDGE : (i + 1) * EDGE].astype(BF16) for i in range(4)]


def apply_once(edge_ref, map_refs, source, target, leaves=range(4)):
    position = lax.axis_index("sub") % 4
    for r in leaves:
        for i, value in enumerate(apply_leaf(edge_ref, map_refs, source, r)):
            target[(position ^ r) * 4 + i] = value


def apply_some(edge_ref, map_refs, source, leaves, target):
    for r in leaves:
        for i, value in enumerate(apply_leaf(edge_ref, map_refs, source, r)):
            target[r, i] = value


def apply_first(edge_ref, m_ref, own_ref, r):
    position = lax.axis_index("sub") % 4
    parts = []
    for i in range(4):
        block = edge_ref[0, (position ^ r) * 4 + i]
        rows = own_ref[pl.ds(pl.multiple_of(block % 4 * EDGE, EDGE), EDGE), :]
        parts.append(jnp.where(block // 4 == position, rows, jnp.zeros_like(rows)))
    out = jnp.dot(m_ref[...], jnp.concatenate(parts, 0), preferred_element_type=F32)
    if r == 0:
        out = out + own_ref[...].astype(F32)
    return [out[i * EDGE : (i + 1) * EDGE].astype(BF16) for i in range(4)]


def early_kernel(edge, m0, m1, here, begun):
    for r, m in enumerate((m0, m1)):
        here[r] = m[...].T
        for i, value in enumerate(apply_first(edge, m, m0, r)):
            begun[r, i] = value


def early(edge, own, beside):
    here = pltpu.VMEM((2,) + own.shape, BF16)
    begun = pltpu.VMEM((2, 4, EDGE, own.shape[1]), BF16)
    return call(early_kernel, (here, begun), (own, beside), (), edge)


def merge_first_kernel(edge, m0, m1, m2, m3, begun, out, half, work):
    maps = (m0, m1, m2, m3)
    position = lax.axis_index("sub") % 4
    for r in range(2):
        for i in range(4):
            work[(position ^ r) * 4 + i] = begun[r, i]
    for r, m in ((2, m2), (3, m3)):
        for i, value in enumerate(apply_first(edge, m, m0, r)):
            work[(position ^ r) * 4 + i] = value
    apply_once(edge, maps, work, out)
    apply_some(edge, maps, out, (0, 1), half)


def merge_last_kernel(edge, m0, m1, m2, m3, source, half, out, work, last, sems):
    maps = (m0, m1, m2, m3)
    position = lax.axis_index("sub") % 4
    for r in range(2):
        for i in range(4):
            work[(position ^ r) * 4 + i] = half[r, i]
    apply_once(edge, maps, source, work, (2, 3))
    copies = []
    for r in range(4):
        apply_once(edge, maps, work, last, (r,))
        blocks = pl.ds((position ^ r) * 4, 4)
        copies.append(pltpu.make_async_copy(last.at[blocks], out.at[blocks], sems.at[r]))
        copies[-1].start()
    for copy in copies:
        copy.wait()


def merge_first(edge, maps, begun):
    width = maps[0].shape[0]
    work = pltpu.VMEM((4 * width // EDGE, EDGE, width), BF16)
    half = pltpu.VMEM(begun.shape, BF16)
    return call(merge_first_kernel, (work, half), (*maps, begun), (work,), edge)


def merge_last(edge, maps, source, half):
    return pl.pallas_call(
        merge_last_kernel,
        out_shape=jax.ShapeDtypeStruct(source.shape, BF16),
        in_specs=[SMEM] + [VMEM] * 6,
        out_specs=pl.BlockSpec(memory_space=pltpu.HBM),
        scratch_shapes=[pltpu.VMEM(source.shape, BF16)] * 2 + [pltpu.SemaphoreType.DMA((4,))],
        compiler_params=pltpu.CompilerParams(vmem_limit_bytes=16 << 20),
    )(edge, *maps, source, half)


def per_device(leaf_maps, edge, incoming):
    return steps(leaf_maps[0, 0], edge, incoming[0, 0])


def steps(own, edge, incoming):
    width = own.shape[0]
    across = sub_partner(own, 2)
    edge, own_near, mine = split_rhs(edge, own, incoming)
    beside = sub_partner(own, 1)
    here, begun = early(edge, own_near, beside)
    given = group_exchange(mine)
    opposite = sub_partner(across, 1)
    t2, first = products(here, across, given)
    maps = (own_near, beside, across, opposite)

    def swap(sent):
        far = dom_partner(sent[1], 1)
        return dom_partner(sent[0], 0), far

    *sent, t3 = first_sweep(edge, here, t2, first, opposite, given)
    got = swap(sent)
    merged, half = merge_first(edge, maps, begun)
    sent = next_sweep(edge, here, t2, t3, given, got)
    got = swap(sent)
    merged = merge_last(edge, maps, merged, half)
    mine = join(given, got)
    pieces = [mine[0]]
    for r in (1, 2, 3):
        pieces.append(sub_partner(mine[r], r))
    leaf_out = leaf_product(own_near, pieces)
    return merged.reshape(1, 1, 4 * width, width), leaf_out[None, None]


def solution(mesh):
    placed = (P("dom", "sub", None, None), P("dom", None), P("dom", "sub", None, None))
    return jax.shard_map(
        per_device,
        mesh=mesh,
        in_specs=placed,
        out_specs=(P("dom", "sub", None, None), P("dom", "sub", None, None)),
        check_vma=False,
    )
```

```python
import jax
import jax.numpy as jnp
from jax import lax
from jax.experimental import pallas as pl
from jax.experimental.pallas import tpu as pltpu
from jax.sharding import PartitionSpec as P


KTERMS = 4
EDGE = 128
NT = (((1,), (1,)), ((), ()))
BF16 = jnp.bfloat16
F32 = jnp.float32
VMEM = pl.BlockSpec(memory_space=pltpu.VMEM)
EMPTY = pltpu.VMEM((8, 128), F32)
SMEM = pl.BlockSpec(memory_space=pltpu.SMEM)


def near(value):
    return pltpu.with_memory_space_constraint(value, pltpu.VMEM)


def call(kernel, results, args, scratch=(), edge=None):
    specs = [VMEM] * len(args)
    args = list(args)
    if edge is not None:
        specs, args = [SMEM] + specs, [edge] + args
    many = isinstance(results, tuple)
    made = pl.pallas_call(
        kernel,
        out_shape=results,
        in_specs=specs,
        out_specs=(VMEM,) * len(results) if many else VMEM,
        scratch_shapes=list(scratch),
        compiler_params=pltpu.CompilerParams(vmem_limit_bytes=16 << 20),
    )(*args)
    if many:
        return tuple(near(m) for m in made)
    return near(made) if isinstance(results, type(EMPTY)) else made


def sub_partner(value, mask):
    size = lax.axis_size("sub")
    return near(lax.ppermute(value, "sub", [(i, i ^ mask) for i in range(size)]))


def dom_partner(value, first):
    size = lax.axis_size("dom")
    pairs = []
    for low in range(first, first + size, 2):
        left, right = low % size, (low + 1) % size
        pairs += [(left, right), (right, left)]
    return near(lax.ppermute(value, "dom", pairs))


def group_exchange(value):
    size = lax.axis_size("sub")
    groups = [list(range(g, g + 4)) for g in range(0, size, 4)]
    return near(lax.all_to_all(value, "sub", 0, 0, axis_index_groups=groups))


def split_kernel(edge_in, own_in, x_in, edge_out, own_out, pieces, x_ref, sems):
    fetch = pltpu.make_async_copy(x_in, x_ref, sems.at[0])
    others = [
        pltpu.make_async_copy(edge_in, edge_out, sems.at[1]),
        pltpu.make_async_copy(own_in, own_out, sems.at[2]),
    ]
    for copy in [fetch] + others:
        copy.start()
    fetch.wait()
    turned = x_ref[...].T.astype(BF16)
    width = turned.shape[0] // 4
    for k in range(4):
        for i in range(4):
            pieces[k, i] = turned[k * width : (k + 1) * width, i * EDGE : (i + 1) * EDGE]
    for copy in others:
        copy.wait()


def split_rhs(edge, own, x):
    rows, cols = x.shape
    edge, own, pieces = pl.pallas_call(
        split_kernel,
        out_shape=(
            pltpu.SMEM(edge.shape, jnp.int32),
            pltpu.VMEM(own.shape, BF16),
            pltpu.VMEM((4, rows // EDGE, cols // 4, EDGE), BF16),
        ),
        in_specs=[pl.BlockSpec(memory_space=pltpu.HBM)] * 3,
        out_specs=(SMEM, VMEM, VMEM),
        scratch_shapes=[pltpu.VMEM(x.shape, F32), pltpu.SemaphoreType.DMA((3,))],
        compiler_params=pltpu.CompilerParams(vmem_limit_bytes=16 << 20),
    )(*(pltpu.with_memory_space_constraint(a, pltpu.HBM) for a in (edge, own, x)))
    return pltpu.with_memory_space_constraint(edge, pltpu.SMEM), near(own), near(pieces)


def swapped_in(given, got_a, got_b):
    position, parity = lax.axis_index("sub") % 4, lax.axis_index("dom") % 2

    def block(r, i):
        half, k = i // 2, i % 2
        a, b = got_a[r, k].astype(F32), got_b[r, k].astype(F32)
        even_pick = b if half == 0 else a
        odd_pick = a if half == 0 else b
        return given[position ^ r, i].astype(F32) + jnp.where(parity == 0, even_pick, odd_pick)

    return block


def chain(edge_ref, turned, base_block, store, z_ref, known=()):
    position = lax.axis_index("sub") % 4
    for step in range(KTERMS + 1):
        slot, before = step % 2, (step + 1) % 2
        leaves = [r for r in range(4) if step > 0 or r not in known]
        operands = {}
        for r in leaves:
            parts = []
            for i in range(4):
                part = base_block(r, i)
                if step > 0:
                    part = part + z_ref[before, edge_ref[0, (position ^ r) * 4 + i]]
                parts.append(part.astype(BF16))
            operands[r] = jnp.concatenate(parts, 1)
        outs = {
            r: jnp.dot(operands[r], turned[r][...], preferred_element_type=F32) for r in leaves
        }
        for r in leaves:
            for i in range(4):
                value = outs[r][:, i * EDGE : (i + 1) * EDGE]
                if step == KTERMS:
                    store(r, i, value)
                else:
                    z_ref[slot, (position ^ r) * 4 + i] = value


def send_store(to_a, to_b, parity):
    def store(r, i, value):
        half, k = i // 2, i % 2
        value = value.astype(BF16)

        @pl.when(parity == half)
        def _():
            to_b[r, k] = value

        @pl.when(parity != half)
        def _():
            to_a[r, k] = value

    return store


def products_kernel(here, m2, given, t2, begun):
    position = lax.axis_index("sub") % 4
    t2[...] = m2[...].T
    for r, turned in enumerate((here.at[0], here.at[1], t2)):
        v = jnp.concatenate([given[position ^ r, i] for i in range(4)], 1)
        out = jnp.dot(v, turned[...], preferred_element_type=F32)
        for i in range(4):
            begun[r, i] = out[:, i * EDGE : (i + 1) * EDGE]


def products(here, m2, given):
    t2 = pltpu.VMEM(m2.shape, BF16)
    begun = pltpu.VMEM((3,) + given.shape[1:], F32)
    return call(products_kernel, (t2, begun), (here, m2, given))


def first_sweep_kernel(edge, here, t2, begun, m3, given, to_a, to_b, t3, z):
    position, parity = lax.axis_index("sub") % 4, lax.axis_index("dom") % 2
    t3[...] = m3[...].T
    for r in range(3):
        for i in range(4):
            z[0, (position ^ r) * 4 + i] = begun[r, i]
    base = lambda r, i: given[position ^ r, i].astype(F32)
    turned = (here.at[0], here.at[1], t2, t3)
    chain(edge, turned, base, send_store(to_a, to_b, parity), z, (0, 1, 2))


def next_sweep_kernel(edge, here, t2, t3, given, got_a, got_b, to_a, to_b, v, z):
    parity = lax.axis_index("dom") % 2
    block = swapped_in(given, got_a, got_b)
    for r in range(4):
        for i in range(4):
            v[r, i] = block(r, i).astype(BF16)
    base = lambda r, i: v[r, i].astype(F32)
    turned = (here.at[0], here.at[1], t2, t3)
    chain(edge, turned, base, send_store(to_a, to_b, parity), z)


def first_sweep(edge, here, t2, begun, m3, given):
    _, blocks, width, _ = given.shape
    sent = pltpu.VMEM((4, blocks // 2, width, EDGE), BF16)
    t3 = pltpu.VMEM(m3.shape, BF16)
    z = pltpu.VMEM((2, 4 * blocks, width, EDGE), F32)
    args = (here, t2, begun, m3, given)
    return call(first_sweep_kernel, (sent, sent, t3), args, (z,), edge)


def next_sweep(edge, here, t2, t3, given, got):
    _, blocks, width, _ = given.shape
    sent = pltpu.VMEM((4, blocks // 2, width, EDGE), BF16)
    v = pltpu.VMEM(given.shape, BF16)
    z = pltpu.VMEM((2, 4 * blocks, width, EDGE), F32)
    return call(next_sweep_kernel, (sent, sent), (here, t2, t3, given, *got), (v, z), edge)


def join_kernel(given, got_a, got_b, *out_refs):
    block = swapped_in(given, got_a, got_b)
    for r in range(4):
        for i in range(4):
            out_refs[r][i] = block(r, i).astype(BF16)


def join(given, got):
    return call(join_kernel, (pltpu.VMEM(given.shape[1:], BF16),) * 4, (given, *got))


def leaf_kernel(own, u0, u1, u2, u3, out, turned):
    position = lax.axis_index("sub") % 4
    width = u0.shape[1]
    for r, u in enumerate((u0, u1, u2, u3)):
        rows = pl.ds(pl.multiple_of((position ^ r) * width, width), width)
        for i in range(4):
            turned[rows, i * EDGE : (i + 1) * EDGE] = u[i]
    out[...] = lax.dot_general(own[...], turned[...], NT, preferred_element_type=F32)


def leaf_product(own, pieces):
    blocks, width, _ = pieces[0].shape
    result = jax.ShapeDtypeStruct((own.shape[0], 4 * width), F32)
    turned = pltpu.VMEM((4 * width, blocks * EDGE), BF16)
    return call(leaf_kernel, result, (own, *pieces), (turned,))


def apply_leaf(edge_ref, map_refs, source, r):
    leaf = (lax.axis_index("sub") % 4) ^ r
    operand = jnp.concatenate([source[edge_ref[0, leaf * 4 + i]] for i in range(4)], 0)
    out = jnp.dot(map_refs[r][...], operand, preferred_element_type=F32)
    if r == 0:
        out = out + map_refs[0][...].astype(F32)
    return [out[i * EDGE : (i + 1) * EDGE].astype(BF16) for i in range(4)]


def apply_once(edge_ref, map_refs, source, target, leaves=range(4)):
    position = lax.axis_index("sub") % 4
    for r in leaves:
        for i, value in enumerate(apply_leaf(edge_ref, map_refs, source, r)):
            target[(position ^ r) * 4 + i] = value


def apply_some(edge_ref, map_refs, source, leaves, target):
    for r in leaves:
        for i, value in enumerate(apply_leaf(edge_ref, map_refs, source, r)):
            target[r, i] = value


def apply_first(edge_ref, m_ref, own_ref, r):
    position = lax.axis_index("sub") % 4
    parts = []
    for i in range(4):
        block = edge_ref[0, (position ^ r) * 4 + i]
        rows = own_ref[pl.ds(pl.multiple_of(block % 4 * EDGE, EDGE), EDGE), :]
        parts.append(jnp.where(block // 4 == position, rows, jnp.zeros_like(rows)))
    out = jnp.dot(m_ref[...], jnp.concatenate(parts, 0), preferred_element_type=F32)
    if r == 0:
        out = out + own_ref[...].astype(F32)
    return [out[i * EDGE : (i + 1) * EDGE].astype(BF16) for i in range(4)]


def early_kernel(edge, m0, m1, here, begun):
    for r, m in enumerate((m0, m1)):
        here[r] = m[...].T
        for i, value in enumerate(apply_first(edge, m, m0, r)):
            begun[r, i] = value


def early(edge, own, beside):
    here = pltpu.VMEM((2,) + own.shape, BF16)
    begun = pltpu.VMEM((2, 4, EDGE, own.shape[1]), BF16)
    return call(early_kernel, (here, begun), (own, beside), (), edge)


def merge_first_kernel(edge, m0, m1, m2, m3, begun, out, half, work):
    maps = (m0, m1, m2, m3)
    position = lax.axis_index("sub") % 4
    for r in range(2):
        for i in range(4):
            work[(position ^ r) * 4 + i] = begun[r, i]
    for r, m in ((2, m2), (3, m3)):
        for i, value in enumerate(apply_first(edge, m, m0, r)):
            work[(position ^ r) * 4 + i] = value
    apply_once(edge, maps, work, out)
    apply_some(edge, maps, out, (0, 1), half)


def merge_last_kernel(edge, m0, m1, m2, m3, source, half, out, work, last, sems):
    maps = (m0, m1, m2, m3)
    position = lax.axis_index("sub") % 4
    for r in range(2):
        for i in range(4):
            work[(position ^ r) * 4 + i] = half[r, i]
    apply_once(edge, maps, source, work, (2, 3))
    copies = []
    for r in range(4):
        apply_once(edge, maps, work, last, (r,))
        blocks = pl.ds((position ^ r) * 4, 4)
        copies.append(pltpu.make_async_copy(last.at[blocks], out.at[blocks], sems.at[r]))
        copies[-1].start()
    for copy in copies:
        copy.wait()


def merge_first(edge, maps, begun):
    width = maps[0].shape[0]
    work = pltpu.VMEM((4 * width // EDGE, EDGE, width), BF16)
    half = pltpu.VMEM(begun.shape, BF16)
    return call(merge_first_kernel, (work, half), (*maps, begun), (work,), edge)


def merge_last(edge, maps, source, half):
    return pl.pallas_call(
        merge_last_kernel,
        out_shape=jax.ShapeDtypeStruct(source.shape, BF16),
        in_specs=[SMEM] + [VMEM] * 6,
        out_specs=pl.BlockSpec(memory_space=pltpu.HBM),
        scratch_shapes=[pltpu.VMEM(source.shape, BF16)] * 2 + [pltpu.SemaphoreType.DMA((4,))],
        compiler_params=pltpu.CompilerParams(vmem_limit_bytes=16 << 20),
    )(edge, *maps, source, half)


def per_device(leaf_maps, edge, incoming):
    return steps(leaf_maps[0, 0], edge, incoming[0, 0])


def steps(own, edge, incoming):
    width = own.shape[0]
    across = sub_partner(own, 2)
    edge, own_near, mine = split_rhs(edge, own, incoming)
    beside = sub_partner(own, 1)
    here, begun = early(edge, own_near, beside)
    given = group_exchange(mine)
    opposite = sub_partner(across, 1)
    t2, first = products(here, across, given)
    maps = (own_near, beside, across, opposite)

    def swap(sent):
        far = dom_partner(sent[1], 1)
        return dom_partner(sent[0], 0), far

    *sent, t3 = first_sweep(edge, here, t2, first, opposite, given)
    got = swap(sent)
    merged, half = merge_first(edge, maps, begun)
    sent = next_sweep(edge, here, t2, t3, given, got)
    got = swap(sent)
    merged = merge_last(edge, maps, merged, half)
    mine = join(given, got)
    pieces = [mine[0]]
    for r in (1, 2, 3):
        pieces.append(sub_partner(mine[r], r))
    leaf_out = leaf_product(own_near, pieces)
    return merged.reshape(1, 1, 4 * width, width), leaf_out[None, None]


def solution(mesh):
    placed = (P("dom", "sub", None, None), P("dom", None), P("dom", "sub", None, None))
    return jax.shard_map(
        per_device,
        mesh=mesh,
        in_specs=placed,
        out_specs=(P("dom", "sub", None, None), P("dom", "sub", None, None)),
        check_vma=False,
    )
```
